128 devices in a mesh: snap: 4 (over z_lo, core), pts: 32 (over z_hi, x, y).
Axes of the slice: x: 4, y: 4, z: 4 (z_hi: 2, z_lo: 2; z = z_hi * 2 + z_lo), core: 2. Of those that a mesh axis runs over, the one named last changes fastest.
Arguments:
- strains: bfloat16 [6, 512, 131072], P(None, 'snap', 'pts'), may hold values from -3 to 3
- moduli: float32 [2, 131072], P(None, 'pts'), may hold values from 0.5 to 2
- range_test: bfloat16 [131072, 256], P('pts'), may hold values from -0.015625 to 0.015625
- corange_test: bfloat16 [256, 512], replicated, may hold values from -0.25 to 0.25
- core_left: float32 [512, 512], P(None, 'snap'), may hold values from -0.25 to 0.25
- core_right: bfloat16 [512, 131072], P(None, 'pts'), may hold values from -0.015625 to 0.015625
Outputs:
- range_sketch: float32 [512, 256], P('snap')
- corange_sketch: float32 [256, 131072], P('snap', 'pts')
- core_sketch: float32 [512, 512], replicated
The draws below stay inside these ranges and needn't reach their ends.
All inputs are finite; a program needn't handle non-finite values.
Results may differ from the reference program's by a relative error of at most 0.0031.
Values may be sent and summed in bfloat16 or wider, within the bound.
A program may use at most 64 MiB of HBM per device.

```python
import math
import jax
import jax.numpy as jnp
from jax import lax

K = 256
L = 256
CORE = 512
SNAPS = 512
PTS = 131072


def shard_levels(stream_key, shape, split, smallest, top_value):
    def one(position, blocks):
        heights = jax.random.uniform(jax.random.fold_in(jax.random.fold_in(stream_key, 6), position), (blocks,), jnp.float32, smallest / len(split), top_value / len(split))
        return jnp.repeat(jnp.exp(heights), shape[position] // blocks).reshape((-1,) + (1,) * (len(shape) - position - 1))

    factor_of = one(*split[0])
    for cut in split[1:]:
        factor_of = factor_of * one(*cut)
    return factor_of


def centred(rng, shape, width, limit, cuts=(), dtype=jnp.bfloat16):
    array = width * jax.random.normal(rng, shape, jnp.float32)
    if cuts:
        array = array * shard_levels(rng, shape, cuts, -0.22, 0.18)
    return jnp.clip(array, -limit, limit).astype(dtype)


def setup_inputs(seed: int = 0) -> dict:
    splits = jax.random.split(jax.random.key(seed), 7)
    return {
        "strains": centred(splits[0], (6, SNAPS, PTS), 0.5, 3.0, ((1, 4), (2, 32))),
        "moduli": jnp.clip(jnp.exp(math.log(2.0) - 1.3862944 * jax.random.uniform(splits[1], (2, PTS), jnp.float32) ** shard_levels(splits[1], (2, PTS), ((1, 32),), -0.2, 0.2)), 0.5, 2.0),
        "range_test": centred(splits[2], (PTS, K), PTS ** -0.5, 0.015625, ((0, 32),)),
        "corange_test": centred(splits[3], (L, SNAPS), SNAPS ** -0.5, 0.25),
        "core_left": centred(splits[4], (CORE, SNAPS), SNAPS ** -0.5, 0.25, ((1, 4),), jnp.float32),
        "core_right": centred(splits[5], (CORE, PTS), PTS ** -0.5, 0.015625, ((1, 32),)),
    }


def energy_field(strains, moduli):
    strain_xx = strains[0].astype(jnp.float32)
    strain_yy = strains[1].astype(jnp.float32)
    strain_zz = strains[2].astype(jnp.float32)
    strain_xy = strains[3].astype(jnp.float32)
    strain_yz = strains[4].astype(jnp.float32)
    strain_xz = strains[5].astype(jnp.float32)
    lame_first = moduli[0]
    shear_mod = moduli[1]
    strain_trace = strain_xx + strain_yy + strain_zz
    mean_strain = strain_trace / 3.0
    dev_xx = strain_xx - mean_strain
    dev_yy = strain_yy - mean_strain
    dev_zz = strain_zz - mean_strain
    dev_square = (dev_xx * dev_xx + dev_yy * dev_yy + dev_zz * dev_zz + 2.0 * (strain_xy * strain_xy + strain_yz * strain_yz + strain_xz * strain_xz)) / 6.0
    dev_norm = jnp.sqrt(dev_square)
    dev_det = dev_xx * (dev_yy * dev_zz - strain_yz * strain_yz) - strain_xy * (strain_xy * dev_zz - strain_yz * strain_xz) + strain_xz * (strain_xy * strain_yz - dev_yy * strain_xz)
    sine_part = jnp.sqrt(jnp.maximum(4.0 * dev_square * dev_square * dev_square - dev_det * dev_det, 0.0))
    angle_third = jnp.arctan2(sine_part, dev_det) / 3.0
    positive_trace = jnp.maximum(strain_trace, 0.0)
    density = 0.5 * lame_first * positive_trace * positive_trace
    for order in range(3):
        principal = mean_strain + 2.0 * dev_norm * jnp.cos(angle_third - 2.0 * math.pi * order / 3.0)
        positive = jnp.maximum(principal, 0.0)
        density = density + shear_mod * positive * positive
    return density.astype(jnp.bfloat16)

def reference(strains, moduli, range_test, corange_test, core_left, core_right):

    def one_snapshot(snapshot):
        return energy_field(snapshot, moduli)
    energy = lax.map(one_snapshot, jnp.transpose(strains, (1, 0, 2)))
    range_sketch = jnp.dot(energy, range_test, preferred_element_type=jnp.float32)
    corange_sketch = jnp.dot(corange_test, energy, preferred_element_type=jnp.float32)
    cross_sum = lax.dot_general(energy, core_right, (((1,), (1,)), ((), ())), preferred_element_type=jnp.float32)
    core_sketch = jnp.dot(core_left, cross_sum, precision=lax.Precision.HIGHEST)
    return (range_sketch, corange_sketch, core_sketch)
```

```python
import jax
import jax.numpy as jnp
from jax import lax
from jax.experimental import pallas as pl
from jax.experimental.pallas import tpu as pltpu
from jax.sharding import PartitionSpec as P

MESH = pl.DeviceIdType.MESH
F32 = jnp.float32
BF16 = jnp.bfloat16
NT = (((1,), (1,)), ((), ()))

CHUNK = 512
LANES = 128
ROWS = 16

ROOT = (
    0.5000000055642606,
    0.24999799048045115,
    -0.18738033617581623,
    0.24724082978273138,
    -0.37786422526526064,
    0.5312551787148476,
    -0.5329691265664762,
    0.26064257700530713,
)
TINY = 1e-36

FAR = sorted(
    ((dx, dy) for dx in range(4) for dy in range(4) if (dx, dy) != (0, 0)),
    key=lambda d: -(min(d[0], 4 - d[0]) + min(d[1], 4 - d[1])),
)
COLUMN = [(2, 0), (2, 1), (1, 0), (3, 0), (1, 1), (3, 1), (0, 1)]


def energy_tile(xx, yy, zz, xy, yz, xz, half_lame, shear):
    trace = xx + yy + zz
    mean = trace * (1.0 / 3.0)
    a = xx - mean
    b = yy - mean
    c = zz - mean
    ac = a * c
    d2 = xy * xy
    e2 = yz * yz
    f2 = xz * xz
    j2 = (b * b - ac) + ((d2 + e2) + f2)
    de = xy * yz
    half_det = 0.5 * (b * (ac - f2) - a * e2 - c * d2) + de * xz
    inv = lax.rsqrt(jnp.maximum(j2, TINY))
    norm = j2 * inv
    ratio = (jnp.abs(half_det) * inv) * (inv * inv)
    ratio = ratio + ratio
    root = jnp.full_like(ratio, ROOT[-1])
    for coef in ROOT[-2::-1]:
        root = root * ratio + coef
    outer = norm * root
    rest = jnp.maximum(j2 - 3.0 * (outer * outer), 0.0)
    split = rest * lax.rsqrt(jnp.maximum(rest, TINY))
    outer = jnp.where(half_det < 0.0, -outer, outer)
    lone = jnp.maximum(mean + (outer + outer), 0.0)
    middle = mean - outer
    upper = jnp.maximum(middle + split, 0.0)
    lower = jnp.maximum(middle - split, 0.0)
    squares = lone * lone + upper * upper + lower * lower
    positive = jnp.maximum(trace, 0.0)
    return half_lame * (positive * positive) + shear * squares


def kernel(
    strains_hbm, moduli_hbm, range_hbm, corange_hbm, left_hbm, right_hbm,
    own_hbm, range_out_hbm, core_out_hbm,
    strains, moduli, range_w, right_w, corange_w, left_w, energy,
    cross_acc, range_acc, own_acc, far_acc, pair_send, pair_recv, far_send, far_recv,
    cross_send, cross_recv, range_recv, range_mid, range_zrecv, range_fin, range_all,
    col_send, col_recv, col_piece, col_all, core_all,
    in_sems, w_sems, pair_ssem, pair_rsem, far_ssem, far_rsem,
    plane_sems, range_sems, col_sems, out_sems,
):
    snap = lax.axis_index("snap")
    pts = lax.axis_index("pts")
    z_lo = snap // 2
    core = snap % 2
    z_hi = pts // 16
    x = (pts // 4) % 4
    y = pts % 4
    z = z_hi * 2 + z_lo
    plane = pts % 16
    slot = z * 2 + core

    def in_plane(dx, dy):
        return (x + dx) % 4 * 4 + (y + dy) % 4

    def plane_id(xy):
        return {"snap": snap, "pts": z_hi * 16 + xy}

    def in_column(dz, dc):
        return (z + dz) % 4 * 2 + (core + dc) % 2

    def column_id(q):
        zz = q // 2
        return {"snap": zz % 2 * 2 + q % 2, "pts": zz // 2 * 16 + plane}

    pair = {"snap": z_lo * 2 + (1 - core), "pts": pts}
    far = {"snap": (1 - z_lo) * 2 + core, "pts": pts}

    chunks = strains.shape[0]

    def inputs(j):
        cols = pl.ds(pl.multiple_of(j * CHUNK, CHUNK), CHUNK)
        return (
            pltpu.make_async_copy(strains_hbm.at[:, :, cols], strains.at[j], in_sems.at[0, j]),
            pltpu.make_async_copy(moduli_hbm.at[:, cols], moduli.at[j], in_sems.at[1, j]),
            pltpu.make_async_copy(right_hbm.at[:, cols], right_w.at[j], in_sems.at[2, j]),
            pltpu.make_async_copy(range_hbm.at[cols, :], range_w.at[j], in_sems.at[3, j]),
        )

    weights = []
    own_cols = pl.ds(pl.multiple_of(snap * 128, 128), 128)
    owners = (snap, (1 - z_lo) * 2 + core, z_lo * 2 + (1 - core), (1 - z_lo) * 2 + (1 - core))
    for n, owner in enumerate(owners):
        rows = pl.ds(pl.multiple_of(owner * 64, 64), 64)
        weights.append(
            pltpu.make_async_copy(
                corange_hbm.at[rows, own_cols], corange_w.at[pl.ds(n * 64, 64), :], w_sems.at[n]
            )
        )
    left_copy = pltpu.make_async_copy(left_hbm, left_w, w_sems.at[4])

    for copy in inputs(0):
        copy.start()
    for copy in weights:
        copy.start()

    @pl.loop(1, chunks)
    def _(j):
        for copy in inputs(j):
            copy.start()

    left_copy.start()

    barrier = pltpu.get_barrier_semaphore()
    for dx, dy in FAR:
        pl.semaphore_signal(
            barrier, inc=1, device_id=plane_id(in_plane(dx, dy)), device_id_type=MESH
        )
    for dz, dc in COLUMN:
        pl.semaphore_signal(
            barrier, inc=1, device_id=column_id(in_column(dz, dc)), device_id_type=MESH
        )

    cross_acc[...] = jnp.zeros_like(cross_acc)
    range_acc[...] = jnp.zeros_like(range_acc)
    for copy in weights:
        copy.wait()

    def pair_copy(j):
        return pltpu.make_async_remote_copy(
            src_ref=pair_send.at[j],
            dst_ref=pair_recv.at[j],
            send_sem=pair_ssem.at[j],
            recv_sem=pair_rsem.at[j],
            device_id=pair,
            device_id_type=MESH,
        )

    def far_copy(j):
        return pltpu.make_async_remote_copy(
            src_ref=far_send.at[j],
            dst_ref=far_recv.at[j],
            send_sem=far_ssem.at[j],
            recv_sem=far_rsem.at[j],
            device_id=far,
            device_id_type=MESH,
        )

    def pass_on(j):
        pair_copy(j).wait_recv()
        far_send[j] = (far_acc[j] + pair_recv[j, 1].astype(F32)).astype(BF16)
        far_copy(j).start()
        own_acc[j] = own_acc[j] + pair_recv[j, 0].astype(F32)

    @pl.loop(0, chunks)
    def _(j):
        for copy in inputs(j):
            copy.wait()

        @pl.loop(0, 128 // ROWS)
        def _(i):
            rows = pl.ds(pl.multiple_of(i * ROWS, ROWS), ROWS)
            for lane in range(0, CHUNK, LANES):
                cols = pl.ds(lane, LANES)
                parts = [strains[j, k, rows, cols].astype(F32) for k in range(6)]
                energy[rows, cols] = energy_tile(
                    *parts, 0.5 * moduli[j, 0:1, cols], moduli[j, 1:2, cols]
                ).astype(BF16)

        field = energy[...]
        own = jnp.dot(corange_w[...], field, preferred_element_type=F32)
        own_acc[j] = own[:64]
        far_acc[j] = own[64:128]
        pair_send[j, 0] = own[128:192].astype(BF16)
        pair_send[j, 1] = own[192:].astype(BF16)

        @pl.when(j == 0)
        def _():
            pl.semaphore_wait(barrier, len(FAR) + len(COLUMN))

        pair_copy(j).start()
        cross_acc[...] += lax.dot_general(right_w[j], field, NT, preferred_element_type=F32)
        range_acc[...] += jnp.dot(field, range_w[j], preferred_element_type=F32)

        @pl.when(j > 0)
        def _():
            pass_on(j - 1)

    for n in range(16):
        cross_send[n] = cross_acc[pl.ds(n * 32, 32), :].astype(BF16)
    plane_copies = []
    for n, (dx, dy) in enumerate(FAR):
        xy = in_plane(dx, dy)
        copy = pltpu.make_async_remote_copy(
            src_ref=cross_send.at[xy],
            dst_ref=cross_recv.at[n],
            send_sem=plane_sems.at[0],
            recv_sem=plane_sems.at[1],
            device_id=plane_id(xy),
            device_id_type=MESH,
        )
        copy.start()
    for n, (dx, dy) in enumerate(FAR):
        xy = in_plane(dx, dy)
        copy = pltpu.make_async_remote_copy(
            src_ref=range_acc.at[pl.ds(pl.multiple_of(xy * 8, 8), 8), :],
            dst_ref=range_recv.at[n],
            send_sem=range_sems.at[0],
            recv_sem=range_sems.at[1],
            device_id=plane_id(xy),
            device_id_type=MESH,
        )
        copy.start()

    pass_on(chunks - 1)
    left_copy.wait()

    def everything(ref, sems, device, send, recv):
        whole = pltpu.make_async_remote_copy(
            src_ref=ref,
            dst_ref=ref,
            send_sem=sems.at[send],
            recv_sem=sems.at[recv],
            device_id=device,
            device_id_type=MESH,
        )
        return whole

    some = plane_id(in_plane(1, 0))
    one = column_id(in_column(0, 1))

    everything(cross_recv, plane_sems, some, 0, 1).wait_recv()
    total = cross_acc[pl.ds(pl.multiple_of(plane * 32, 32), 32), :]
    for n in range(15):
        total = total + cross_recv[n].astype(F32)
    share = lax.dot_general(
        total, left_w[...], NT, precision=lax.Precision.HIGHEST, preferred_element_type=F32
    )
    for q in range(8):
        half, block = q // 4, q % 4
        col_send[q] = share[half * 16 : half * 16 + 16, block * 128 : block * 128 + 128]
    for n, (dz, dc) in enumerate(COLUMN):
        q = in_column(dz, dc)
        pltpu.make_async_remote_copy(
            src_ref=col_send.at[q],
            dst_ref=col_recv.at[n],
            send_sem=col_sems.at[0],
            recv_sem=col_sems.at[1],
            device_id=column_id(q),
            device_id_type=MESH,
        ).start()

    everything(range_recv, range_sems, some, 0, 1).wait_recv()
    part = range_acc[pl.ds(pl.multiple_of(plane * 8, 8), 8), :]
    for n in range(15):
        part = part + range_recv[n]
    range_mid[...] = part
    z_copy = pltpu.make_async_remote_copy(
        src_ref=range_mid,
        dst_ref=range_zrecv,
        send_sem=range_sems.at[2],
        recv_sem=range_sems.at[3],
        device_id=column_id(in_column(2, 0)),
        device_id_type=MESH,
    )
    z_copy.start()

    everything(col_recv, col_sems, one, 0, 1).wait_recv()
    piece = col_send[slot]
    for n in range(7):
        piece = piece + col_recv[n]
    col_piece[...] = piece.astype(BF16)
    for dz, dc in COLUMN:
        q = in_column(dz, dc)
        pltpu.make_async_remote_copy(
            src_ref=col_piece,
            dst_ref=col_all.at[slot],
            send_sem=col_sems.at[2],
            recv_sem=col_sems.at[3],
            device_id=column_id(q),
            device_id_type=MESH,
        ).start()
    mine = pltpu.make_async_copy(col_piece, col_all.at[slot], col_sems.at[3])
    mine.start()

    z_copy.wait_recv()
    range_fin[...] = part + range_zrecv[...]

    everything(col_all, col_sems, one, 2, 3).wait_recv()
    for dx, dy in FAR:
        pltpu.make_async_remote_copy(
            src_ref=col_all,
            dst_ref=core_all.at[plane],
            send_sem=plane_sems.at[2],
            recv_sem=plane_sems.at[3],
            device_id=plane_id(in_plane(dx, dy)),
            device_id_type=MESH,
        ).start()
    pltpu.make_async_copy(col_all, core_all.at[plane], plane_sems.at[3]).start()
    for dx, dy in FAR:
        pltpu.make_async_remote_copy(
            src_ref=range_fin,
            dst_ref=range_all.at[plane],
            send_sem=range_sems.at[4],
            recv_sem=range_sems.at[5],
            device_id=plane_id(in_plane(dx, dy)),
            device_id_type=MESH,
        ).start()
    pltpu.make_async_copy(range_fin, range_all.at[plane], range_sems.at[5]).start()

    def own_copy(j):
        cols = pl.ds(pl.multiple_of(j * CHUNK, CHUNK), CHUNK)
        return pltpu.make_async_copy(own_acc.at[j], own_hbm.at[:, cols], out_sems.at[j])

    @pl.loop(0, chunks)
    def _(j):
        far_copy(j).wait_recv()
        own_acc[j] = own_acc[j] + far_recv[j].astype(F32)
        own_copy(j).start()

    everything(range_all, range_sems, some, 4, 5).wait_recv()
    range_copy = pltpu.make_async_copy(range_all, range_out_hbm, out_sems.at[chunks])
    range_copy.start()
    everything(core_all, plane_sems, some, 2, 3).wait_recv()
    core_copy = pltpu.make_async_copy(core_all, core_out_hbm, out_sems.at[chunks + 1])
    core_copy.start()

    everything(cross_recv, plane_sems, some, 0, 1).wait_send()
    everything(range_recv, range_sems, some, 0, 1).wait_send()
    everything(range_mid, range_sems, some, 2, 3).wait_send()
    everything(col_recv, col_sems, one, 0, 1).wait_send()
    everything(col_all.at[pl.ds(0, 7)], col_sems, one, 2, 3).wait_send()
    everything(core_all.at[pl.ds(0, 15)], plane_sems, some, 2, 3).wait_send()
    everything(range_all.at[pl.ds(0, 15)], range_sems, some, 4, 5).wait_send()

    @pl.loop(0, chunks)
    def _(j):
        pair_copy(j).wait_send()
        far_copy(j).wait_send()
        own_copy(j).wait()

    range_copy.wait()
    core_copy.wait()


def per_device(strains, moduli, range_test, corange_test, core_left, core_right):
    points = strains.shape[2]
    chunks = points // CHUNK
    any_spec = pl.BlockSpec(memory_space=pl.ANY)
    dma = pltpu.SemaphoreType.DMA
    vmem = pltpu.VMEM
    own, range_all, core_all = pl.pallas_call(
        kernel,
        out_shape=(
            jax.ShapeDtypeStruct((64, points), F32),
            jax.ShapeDtypeStruct((16, 8, 256), F32),
            jax.ShapeDtypeStruct((16, 8, 16, 128), BF16),
        ),
        in_specs=[any_spec] * 6,
        out_specs=(any_spec,) * 3,
        scratch_shapes=[
            vmem((chunks, 6, 128, CHUNK), BF16),
            vmem((chunks, 2, CHUNK), F32),
            vmem((chunks, CHUNK, 256), BF16),
            vmem((chunks, 512, CHUNK), BF16),
            vmem((256, 128), BF16),
            vmem((512, 128), F32),
            vmem((128, CHUNK), BF16),
            vmem((512, 128), F32),
            vmem((128, 256), F32),
            vmem((chunks, 64, CHUNK), F32),
            vmem((chunks, 64, CHUNK), F32),
            vmem((chunks, 2, 64, CHUNK), BF16),
            vmem((chunks, 2, 64, CHUNK), BF16),
            vmem((chunks, 64, CHUNK), BF16),
            vmem((chunks, 64, CHUNK), BF16),
            vmem((16, 32, 128), BF16),
            vmem((15, 32, 128), BF16),
            vmem((15, 8, 256), F32),
            vmem((8, 256), F32),
            vmem((8, 256), F32),
            vmem((8, 256), F32),
            vmem((16, 8, 256), F32),
            vmem((8, 16, 128), F32),
            vmem((7, 16, 128), F32),
            vmem((16, 128), BF16),
            vmem((8, 16, 128), BF16),
            vmem((16, 8, 16, 128), BF16),
            dma((4, chunks)),
            dma((5,)),
            dma((chunks,)),
            dma((chunks,)),
            dma((chunks,)),
            dma((chunks,)),
            dma((4,)),
            dma((6,)),
            dma((4,)),
            dma((chunks + 2,)),
        ],
        compiler_params=pltpu.CompilerParams(collective_id=0, has_side_effects=True),
    )(strains, moduli, range_test, corange_test, core_left, core_right)
    core = core_all.reshape(16, 2, 4, 16, 128).transpose(2, 4, 0, 1, 3).reshape(512, 512)
    return range_all.reshape(128, 256), own, core.astype(F32)


def solution(mesh):
    in_specs = (
        P(None, "snap", "pts"),
        P(None, "pts"),
        P("pts", None),
        P(),
        P(None, "snap"),
        P(None, "pts"),
    )
    out_specs = (P("snap", None), P("snap", "pts"), P())
    return jax.shard_map(
        per_device, mesh=mesh, in_specs=in_specs, out_specs=out_specs, check_vma=False
    )
```

```python
import jax
import jax.numpy as jnp
from jax import lax
from jax.experimental import pallas as pl
from jax.experimental.pallas import tpu as pltpu
from jax.sharding import PartitionSpec as P

MESH = pl.DeviceIdType.MESH
F32 = jnp.float32
BF16 = jnp.bfloat16
NT = (((1,), (1,)), ((), ()))

CHUNK = 512
START = 3
HOLD = 3

ROOT = (
    0.5000000397996354,
    2 * 0.2499888951698186,
    -4 * 0.18699047969551208,
    8 * 0.24102109068796812,
    -16 * 0.3308495451729968,
    32 * 0.3494727775510849,
    -64 * 0.18534731636945423,
)
TINY = 1e-36


def hops(d):
    return sum(min(v, 4 - v) for v in d[:3])


OTHERS = sorted(
    (
        (dx, dy, dz, dc)
        for dx in range(4)
        for dy in range(4)
        for dz in range(4)
        for dc in range(2)
        if (dx, dy, dz, dc) != (0, 0, 0, 0)
    ),
    key=hops,
    reverse=True,
)
SAME_CORE = [d for d in OTHERS if d[3] == 0]
SAME_SNAP = [d for d in SAME_CORE if d[2] in (0, 2)]


def energy_tile(xx, yy, zz, xy, yz, xz, half_lame, shear):
    trace = xx + yy + zz
    mean = trace * (1.0 / 3.0)
    a = xx - mean
    b = yy - mean
    c = zz - mean
    ac = a * c
    d2 = xy * xy
    e2 = yz * yz
    f2 = xz * xz
    j2 = jnp.maximum((b * b - ac) + ((d2 + e2) + f2), TINY)
    half_det = 0.5 * (b * (ac - f2) - (a * e2 + c * d2)) + (xy * yz) * xz
    inv = lax.rsqrt(j2)
    ratio = (jnp.abs(half_det) * inv) * (inv * inv)
    root = jnp.full_like(ratio, ROOT[-1])
    for coef in ROOT[-2::-1]:
        root = root * ratio + coef
    outer = (j2 * inv) * root
    rest = jnp.maximum(j2 - 3.0 * (outer * outer), TINY)
    split = rest * lax.rsqrt(rest)
    outer = jnp.where(half_det < 0.0, -outer, outer)
    middle = mean - outer
    lone = jnp.maximum(mean + (outer + outer), 0.0)
    upper = jnp.maximum(middle + split, 0.0)
    lower = jnp.maximum(middle - split, 0.0)
    positive = jnp.maximum(trace, 0.0)
    squares = lone * lone + upper * upper + lower * lower
    return half_lame * (positive * positive) + shear * squares


def kernel(
    strains_hbm, moduli_hbm, range_hbm, corange_hbm, left_hbm, right_hbm,
    own_hbm, range_out_hbm, core_out_hbm,
    strains, moduli, range_w, right_w, corange_w, left_w, left_all, energy,
    cross_acc, range_acc, own_acc, far_acc, pair_send, pair_recv, far_send, far_recv,
    cross_send, cross_recv, range_send, range_recv, range_piece, range_all, range_sum,
    core_piece, core_all, order, core_sum,
    in_sems, w_sems, pair_ssem, pair_rsem, far_ssem, far_rsem,
    left_sems, cross_sems, range_sems, core_sems, out_sems,
):
    snap = lax.axis_index("snap")
    pts = lax.axis_index("pts")
    z_lo = snap // 2
    core = snap % 2
    z = pts // 16 * 2 + z_lo
    x = (pts // 4) % 4
    y = pts % 4

    def place(d):
        zz = (z + d[2]) % 4
        to_snap = zz % 2 * 2 + (core + d[3]) % 2
        return to_snap, zz // 2 * 16 + (x + d[0]) % 4 * 4 + (y + d[1]) % 4

    def device(where):
        return {"snap": where[0], "pts": where[1]}

    pair = (z_lo * 2 + (1 - core), pts)
    far_snap = (1 - z_lo) * 2 + core
    far = (far_snap, pts)
    outer_z = (z + 3 + 2 * z_lo) % 4
    outer = (far_snap, outer_z // 2 * 16 + pts % 16)

    def remote(src, dst, sems, send, recv, where):
        return pltpu.make_async_remote_copy(
            src_ref=src,
            dst_ref=dst,
            send_sem=sems.at[send],
            recv_sem=sems.at[recv],
            device_id=device(where),
            device_id_type=MESH,
        )

    chunks = strains.shape[0]

    def inputs(j):
        cols = pl.ds(pl.multiple_of(j * CHUNK, CHUNK), CHUNK)
        return (
            pltpu.make_async_copy(strains_hbm.at[:, :, cols], strains.at[j], in_sems.at[0, j]),
            pltpu.make_async_copy(moduli_hbm.at[:, cols], moduli.at[j], in_sems.at[1, j]),
            pltpu.make_async_copy(right_hbm.at[:, cols], right_w.at[j], in_sems.at[2, j]),
            pltpu.make_async_copy(range_hbm.at[cols, :], range_w.at[j], in_sems.at[3, j]),
        )

    weights = []
    own_cols = pl.ds(pl.multiple_of(snap * 128, 128), 128)
    pair_far = (1 - z_lo) * 2 + (1 - core)
    for n, owner in enumerate((snap, far_snap, pair[0], pair_far)):
        rows = pl.ds(pl.multiple_of(owner * 64, 64), 64)
        weights.append(
            pltpu.make_async_copy(
                corange_hbm.at[rows, own_cols], corange_w.at[pl.ds(n * 64, 64), :], w_sems.at[n]
            )
        )
    left_copy = pltpu.make_async_copy(left_hbm, left_w, w_sems.at[4])

    for copy in inputs(0):
        copy.start()
    left_copy.start()
    for copy in weights:
        copy.start()

    @pl.loop(1, chunks)
    def _(j):
        for copy in inputs(j):
            copy.start()

    barrier = pltpu.get_barrier_semaphore()
    me = snap * 32 + pts

    @pl.loop(1, 128)
    def _(n):
        other = (me + n) % 128
        pl.semaphore_signal(
            barrier, inc=1, device_id=device((other // 32, other % 32)), device_id_type=MESH
        )

    cross_acc[...] = jnp.zeros_like(cross_acc)
    range_acc[...] = jnp.zeros_like(range_acc)

    def pair_copy(j):
        return pltpu.make_async_remote_copy(
            src_ref=pair_send.at[j],
            dst_ref=pair_recv.at[j],
            send_sem=pair_ssem.at[j],
            recv_sem=pair_rsem.at[j],
            device_id=device(pair),
            device_id_type=MESH,
        )

    def far_copy(j):
        return pltpu.make_async_remote_copy(
            src_ref=far_send.at[j],
            dst_ref=far_recv.at[j],
            send_sem=far_ssem.at[j],
            recv_sem=far_rsem.at[j],
            device_id=device(far),
            device_id_type=MESH,
        )

    def pass_on(j):
        pair_copy(j).wait_recv()
        far_send[j] = (far_acc[j] + pair_recv[j, 1].astype(F32)).astype(BF16)
        far_copy(j).start()

    def energies(j):
        for lane in range(0, CHUNK, 128):
            cols = pl.ds(lane, 128)
            half_lame = 0.5 * moduli[j, 0:1, cols]
            shear = moduli[j, 1:2, cols]
            for row in range(0, 128, 16):
                rows = pl.ds(row, 16)
                parts = [strains[j, k, rows, cols].astype(F32) for k in range(6)]
                energy[j, rows, cols] = energy_tile(*parts, half_lame, shear).astype(BF16)

    def products(j):
        field = energy[j]
        own = jnp.dot(corange_w[...], field, preferred_element_type=F32)
        own_acc[j] = own[:64]
        far_acc[j] = own[64:128]
        pair_send[j, 0] = own[128:192].astype(BF16)
        pair_send[j, 1] = own[192:].astype(BF16)
        cross_acc[...] += lax.dot_general(right_w[j], field, NT, preferred_element_type=F32)
        range_acc[...] += jnp.dot(field, range_w[j], preferred_element_type=F32)

    def left_slot(s):
        return left_all.at[:, :, pl.ds(pl.multiple_of(s * 128, 128), 128)]

    def left_pair():
        return remote(left_slot(snap), left_slot(snap), left_sems, 0, 1, pair)

    def left_outer():
        return remote(left_slot(snap), left_slot(snap), left_sems, 2, 3, outer)

    def left_relay():
        return remote(left_slot(far_snap), left_slot(far_snap), left_sems, 4, 5, pair)

    for copy in inputs(0):
        copy.wait()
    energies(0)
    for copy in weights:
        copy.wait()
    left_copy.wait()
    left = left_w[...]
    left_top = left.astype(BF16)
    left_all[0, :, own_cols] = left_top
    left_all[1, :, own_cols] = (left - left_top.astype(F32)).astype(BF16)

    @pl.loop(1, chunks)
    def _(j):
        for copy in inputs(j):
            copy.wait()
        products(j - 1)
        energies(j)

        @pl.when(j == START)
        def _():
            pl.semaphore_wait(barrier, 127)
            left_outer().start()
            left_pair().start()
            for i in range(START - 1):
                pair_copy(i).start()

        @pl.when(j >= START)
        def _():
            pair_copy(j - 1).start()

        @pl.when((j > START) & (j <= START + HOLD))
        def _():
            pass_on(j - START - 1)

    products(chunks - 1)

    for n in range(128):
        cross_send[n] = cross_acc[pl.ds(n * 4, 4), :].astype(BF16)
    for d in OTHERS:
        where = place(d)
        remote(
            cross_send.at[where[0] * 32 + where[1]], cross_recv.at[snap, pts], cross_sems, 0, 1, where
        ).start()
    pltpu.make_async_copy(cross_send.at[me], cross_recv.at[snap, pts], cross_sems.at[1]).start()

    for n in range(32):
        rows, cols = pl.ds(n // 2 * 8, 8), pl.ds(n % 2 * 128, 128)
        range_send[n] = range_acc[rows, cols].astype(BF16)
    for d in SAME_SNAP:
        where = place(d)
        remote(range_send.at[where[1]], range_recv.at[pts], range_sems, 0, 1, where).start()
    pltpu.make_async_copy(range_send.at[pts], range_recv.at[pts], range_sems.at[1]).start()

    pair_copy(chunks - 1).start()
    done = min(HOLD, chunks - 1 - START)
    left_outer().wait_recv()
    left_relay().start()

    @pl.loop(done, chunks)
    def _(j):
        pass_on(j)

    row = lax.broadcasted_iota(jnp.int32, (512, 512), 0)
    col = lax.broadcasted_iota(jnp.int32, (512, 512), 1)
    source = (col & 127) // 4 * 16 + col // 128 * 4 + (col & 3)
    order[...] = jnp.where(row == source, 1.0, 0.0).astype(BF16)

    left_pair().wait_recv()
    left_relay().wait_recv()

    remote(cross_recv, cross_recv, cross_sems, 0, 1, pair).wait_recv()
    total = jnp.concatenate([jnp.sum(cross_recv[s].astype(F32), axis=0) for s in range(4)], axis=1)
    low = total - total.astype(BF16).astype(F32)
    both = jnp.concatenate([total, low], axis=0).astype(BF16)
    top = lax.dot_general(both, left_all[0], NT, preferred_element_type=F32)
    bottom = lax.dot_general(both, left_all[1], NT, preferred_element_type=F32)
    share = top[0:4] + (top[4:8] + bottom[0:4])
    core_piece[...] = jnp.concatenate(
        [share[:, k * 128 : k * 128 + 128] for k in range(4)], axis=0
    ).astype(BF16)
    slot = z_lo * 32 + pts
    for d in SAME_CORE:
        remote(core_piece, core_all.at[core, slot], core_sems, 0, 1, place(d)).start()
    pltpu.make_async_copy(core_piece, core_all.at[core, slot], core_sems.at[1]).start()

    remote(range_recv, range_recv, range_sems, 0, 1, pair).wait_recv()
    range_piece[...] = jnp.sum(range_recv[...].astype(F32), axis=0).astype(BF16)
    for d in SAME_SNAP:
        remote(range_piece, range_all.at[pts], range_sems, 2, 3, place(d)).start()
    pltpu.make_async_copy(range_piece, range_all.at[pts], range_sems.at[3]).start()

    def own_copy(j):
        cols = pl.ds(pl.multiple_of(j * CHUNK, CHUNK), CHUNK)
        return pltpu.make_async_copy(own_acc.at[j], own_hbm.at[:, cols], out_sems.at[j])

    @pl.loop(0, chunks)
    def _(j):
        far_copy(j).wait_recv()
        own_acc[j] = own_acc[j] + pair_recv[j, 0].astype(F32) + far_recv[j].astype(F32)
        own_copy(j).start()

    remote(core_all.at[core], core_all.at[core], core_sems, 0, 1, pair).wait_recv()
    relay = remote(core_all.at[core], core_all.at[core], core_sems, 2, 3, pair)
    relay.start()

    def arrange(which):
        for half in range(2):
            block = core_all[which, pl.ds(half * 32, 32)].reshape(512, 128)
            turned = lax.dot_general(
                block, order[...], (((0,), (0,)), ((), ())), preferred_element_type=F32
            ).astype(BF16)
            cols = pl.ds(pl.multiple_of((half * 2 + which) * 128, 128), 128)
            for k in range(4):
                core_sum[pl.ds(k * 128, 128), cols] = turned[:, k * 128 : k * 128 + 128]

    arrange(core)
    remote(range_all, range_all, range_sems, 2, 3, pair).wait_recv()
    for n in range(32):
        rows, cols = pl.ds(n // 2 * 8, 8), pl.ds(n % 2 * 128, 128)
        range_sum[rows, cols] = range_all[n].astype(F32)
    range_copy = pltpu.make_async_copy(range_sum, range_out_hbm, out_sems.at[chunks])
    range_copy.start()
    relay.wait_recv()
    arrange(1 - core)
    core_copy = pltpu.make_async_copy(core_sum, core_out_hbm, out_sems.at[chunks + 1])
    core_copy.start()

    left_outer().wait_send()
    left_pair().wait_send()
    left_relay().wait_send()
    sent = cross_send.at[pl.ds(0, 127)]
    remote(sent, sent, cross_sems, 0, 1, pair).wait_send()
    sent = range_send.at[pl.ds(0, 31)]
    remote(sent, sent, range_sems, 0, 1, pair).wait_send()
    remote(sent, sent, range_sems, 2, 3, pair).wait_send()
    sent = core_all.at[0, pl.ds(0, 63)]
    remote(sent, sent, core_sems, 0, 1, pair).wait_send()
    relay.wait_send()

    @pl.loop(0, chunks)
    def _(j):
        pair_copy(j).wait_send()
        far_copy(j).wait_send()
        own_copy(j).wait()

    range_copy.wait()
    core_copy.wait()


def per_device(strains, moduli, range_test, corange_test, core_left, core_right):
    points = strains.shape[2]
    chunks = points // CHUNK
    any_spec = pl.BlockSpec(memory_space=pl.ANY)
    dma = pltpu.SemaphoreType.DMA
    vmem = pltpu.VMEM
    own, range_sum, core = pl.pallas_call(
        kernel,
        out_shape=(
            jax.ShapeDtypeStruct((64, points), F32),
            jax.ShapeDtypeStruct((128, 256), F32),
            jax.ShapeDtypeStruct((512, 512), BF16),
        ),
        in_specs=[any_spec] * 6,
        out_specs=(any_spec,) * 3,
        scratch_shapes=[
            vmem((chunks, 6, 128, CHUNK), BF16),
            vmem((chunks, 2, CHUNK), F32),
            vmem((chunks, CHUNK, 256), BF16),
            vmem((chunks, 512, CHUNK), BF16),
            vmem((256, 128), BF16),
            vmem((512, 128), F32),
            vmem((2, 512, 512), BF16),
            vmem((chunks, 128, CHUNK), BF16),
            vmem((512, 128), F32),
            vmem((128, 256), F32),
            vmem((chunks, 64, CHUNK), F32),
            vmem((chunks, 64, CHUNK), F32),
            vmem((chunks, 2, 64, CHUNK), BF16),
            vmem((chunks, 2, 64, CHUNK), BF16),
            vmem((chunks, 64, CHUNK), BF16),
            vmem((chunks, 64, CHUNK), BF16),
            vmem((128, 4, 128), BF16),
            vmem((4, 32, 4, 128), BF16),
            vmem((32, 8, 128), BF16),
            vmem((32, 8, 128), BF16),
            vmem((8, 128), BF16),
            vmem((32, 8, 128), BF16),
            vmem((128, 256), F32),
            vmem((16, 128), BF16),
            vmem((2, 64, 16, 128), BF16),
            vmem((512, 512), BF16),
            vmem((512, 512), BF16),
            dma((4, chunks)),
            dma((5,)),
            dma((chunks,)),
            dma((chunks,)),
            dma((chunks,)),
            dma((chunks,)),
            dma((6,)),
            dma((2,)),
            dma((4,)),
            dma((4,)),
            dma((chunks + 2,)),
        ],
        compiler_params=pltpu.CompilerParams(collective_id=0, has_side_effects=True),
    )(strains, moduli, range_test, corange_test, core_left, core_right)
    return range_sum, own, core.astype(F32)


def solution(mesh):
    in_specs = (
        P(None, "snap", "pts"),
        P(None, "pts"),
        P("pts", None),
        P(),
        P(None, "snap"),
        P(None, "pts"),
    )
    out_specs = (P("snap", None), P("snap", "pts"), P())
    return jax.shard_map(
        per_device, mesh=mesh, in_specs=in_specs, out_specs=out_specs, check_vma=False
    )
```

```python
import jax
import jax.numpy as jnp
from jax import lax
from jax.experimental import pallas as pl
from jax.experimental.pallas import tpu as pltpu
from jax.sharding import PartitionSpec as P

MESH = pl.DeviceIdType.MESH
F32 = jnp.float32
BF16 = jnp.bfloat16
NT = (((1,), (1,)), ((), ()))

CHUNK = 512
START = 3
CROSSING = (4, 4, 5, 6, 7, 8, 8, 8)

ROOT = (
    0.5000000397996354,
    2 * 0.2499888951698186,
    -4 * 0.18699047969551208,
    8 * 0.24102109068796812,
    -16 * 0.3308495451729968,
    32 * 0.3494727775510849,
    -64 * 0.18534731636945423,
)
TINY = 1e-36


def hops(d):
    return sum(min(v, 4 - v) for v in d[:3])


OTHERS = sorted(
    (
        (dx, dy, dz, dc)
        for dx in range(4)
        for dy in range(4)
        for dz in range(4)
        for dc in range(2)
        if (dx, dy, dz, dc) != (0, 0, 0, 0)
    ),
    key=hops,
    reverse=True,
)
SAME_CORE = [d for d in OTHERS if d[3] == 0]
SAME_SNAP = [d for d in SAME_CORE if d[2] in (0, 2)]


def energy_tile(xx, yy, zz, xy, yz, xz, half_lame, shear):
    trace = xx + yy + zz
    mean = trace * (1.0 / 3.0)
    a = xx - mean
    b = yy - mean
    c = zz - mean
    ac = a * c
    d2 = xy * xy
    e2 = yz * yz
    f2 = xz * xz
    j2 = jnp.maximum((b * b - ac) + ((d2 + e2) + f2), TINY)
    half_det = 0.5 * (b * (ac - f2) - (a * e2 + c * d2)) + (xy * yz) * xz
    inv = lax.rsqrt(j2)
    ratio = (jnp.abs(half_det) * inv) * (inv * inv)
    root = jnp.full_like(ratio, ROOT[-1])
    for coef in ROOT[-2::-1]:
        root = root * ratio + coef
    outer = (j2 * inv) * root
    rest = jnp.maximum(j2 - 3.0 * (outer * outer), TINY)
    split = rest * lax.rsqrt(rest)
    outer = jnp.where(half_det < 0.0, -outer, outer)
    middle = mean - outer
    lone = jnp.maximum(mean + (outer + outer), 0.0)
    upper = jnp.maximum(middle + split, 0.0)
    lower = jnp.maximum(middle - split, 0.0)
    positive = jnp.maximum(trace, 0.0)
    squares = lone * lone + upper * upper + lower * lower
    return half_lame * (positive * positive) + shear * squares


def kernel(
    strains_hbm, moduli_hbm, range_hbm, corange_hbm, left_hbm, right_hbm,
    own_acc, range_sum, core_sum,
    strains, moduli, range_w, right_w, corange_w, left_w, left_all, energy,
    cross_acc, range_acc, far_acc, pair_send, pair_recv, far_send, far_recv,
    cross_send, cross_recv, range_send, range_recv, range_piece, range_all,
    core_piece, core_all, order,
    in_sems, w_sems, pair_ssem, pair_rsem, far_ssem, far_rsem,
    left_sems, cross_sems, range_sems, core_sems,
):
    snap = lax.axis_index("snap")
    pts = lax.axis_index("pts")
    z_lo = snap // 2
    core = snap % 2
    z = pts // 16 * 2 + z_lo
    x = (pts // 4) % 4
    y = pts % 4

    def place(d):
        zz = (z + d[2]) % 4
        to_snap = zz % 2 * 2 + (core + d[3]) % 2
        return to_snap, zz // 2 * 16 + (x + d[0]) % 4 * 4 + (y + d[1]) % 4

    def device(where):
        return {"snap": where[0], "pts": where[1]}

    pair = (z_lo * 2 + (1 - core), pts)
    far_snap = (1 - z_lo) * 2 + core
    far = (far_snap, pts)
    outer_z = (z + 3 + 2 * z_lo) % 4
    outer = (far_snap, outer_z // 2 * 16 + pts % 16)

    def remote(src, dst, sems, send, recv, where):
        return pltpu.make_async_remote_copy(
            src_ref=src,
            dst_ref=dst,
            send_sem=sems.at[send],
            recv_sem=sems.at[recv],
            device_id=device(where),
            device_id_type=MESH,
        )

    chunks = strains.shape[0]

    def columns(j):
        return pl.ds(pl.multiple_of(j * CHUNK, CHUNK), CHUNK)

    def inputs(j):
        cols = columns(j)
        return (
            pltpu.make_async_copy(strains_hbm.at[:, :, cols], strains.at[j], in_sems.at[0, j]),
            pltpu.make_async_copy(moduli_hbm.at[:, cols], moduli.at[j], in_sems.at[1, j]),
            pltpu.make_async_copy(right_hbm.at[:, cols], right_w.at[j], in_sems.at[2, j]),
            pltpu.make_async_copy(range_hbm.at[cols, :], range_w.at[j], in_sems.at[3, j]),
        )

    weights = []
    own_cols = pl.ds(pl.multiple_of(snap * 128, 128), 128)
    pair_far = (1 - z_lo) * 2 + (1 - core)
    for n, owner in enumerate((snap, far_snap, pair[0], pair_far)):
        rows = pl.ds(pl.multiple_of(owner * 64, 64), 64)
        weights.append(
            pltpu.make_async_copy(
                corange_hbm.at[rows, own_cols], corange_w.at[pl.ds(n * 64, 64), :], w_sems.at[n]
            )
        )
    left_copy = pltpu.make_async_copy(left_hbm, left_w, w_sems.at[4])

    for copy in inputs(0):
        copy.start()
    left_copy.start()
    for copy in weights:
        copy.start()

    @pl.loop(1, chunks)
    def _(j):
        for copy in inputs(j):
            copy.start()

    barrier = pltpu.get_barrier_semaphore()
    me = snap * 32 + pts

    @pl.loop(1, 128)
    def _(n):
        other = (me + n) % 128
        pl.semaphore_signal(
            barrier, inc=1, device_id=device((other // 32, other % 32)), device_id_type=MESH
        )

    cross_acc[...] = jnp.zeros_like(cross_acc)
    range_acc[...] = jnp.zeros_like(range_acc)

    def pair_copy(j):
        return pltpu.make_async_remote_copy(
            src_ref=pair_send.at[j],
            dst_ref=pair_recv.at[j],
            send_sem=pair_ssem.at[j],
            recv_sem=pair_rsem.at[j],
            device_id=device(pair),
            device_id_type=MESH,
        )

    def far_copy(j):
        return pltpu.make_async_remote_copy(
            src_ref=far_send.at[j],
            dst_ref=far_recv.at[j],
            send_sem=far_ssem.at[j],
            recv_sem=far_rsem.at[j],
            device_id=device(far),
            device_id_type=MESH,
        )

    def pass_on(j):
        pair_copy(j).wait_recv()
        far_send[j] = (far_acc[j] + pair_recv[j, 1].astype(F32)).astype(BF16)
        far_copy(j).start()

    def energies(j):
        for lane in range(0, CHUNK, 128):
            cols = pl.ds(lane, 128)
            half_lame = 0.5 * moduli[j, 0:1, cols]
            shear = moduli[j, 1:2, cols]
            for row in range(0, 128, 16):
                rows = pl.ds(row, 16)
                parts = [strains[j, k, rows, cols].astype(F32) for k in range(6)]
                energy[j, rows, cols] = energy_tile(*parts, half_lame, shear).astype(BF16)

    def cross_product(j):
        cross_acc[...] += lax.dot_general(right_w[j], energy[j], NT, preferred_element_type=F32)

    def other_products(j):
        field = energy[j]
        own = jnp.dot(corange_w[...], field, preferred_element_type=F32)
        own_acc[:, columns(j)] = own[:64]
        far_acc[j] = own[64:128]
        pair_send[j, 0] = own[128:192].astype(BF16)
        pair_send[j, 1] = own[192:].astype(BF16)
        range_acc[...] += jnp.dot(field, range_w[j], preferred_element_type=F32)

    def left_slot(s):
        return left_all.at[:, :, pl.ds(pl.multiple_of(s * 128, 128), 128)]

    def left_pair():
        return remote(left_slot(snap), left_slot(snap), left_sems, 0, 1, pair)

    def left_outer():
        return remote(left_slot(snap), left_slot(snap), left_sems, 2, 3, outer)

    def left_relay():
        return remote(left_slot(far_snap), left_slot(far_snap), left_sems, 4, 5, pair)

    for copy in inputs(0):
        copy.wait()
    energies(0)
    for copy in weights:
        copy.wait()
    left_copy.wait()
    left = left_w[...]
    left_top = left.astype(BF16)
    left_all[0, :, own_cols] = left_top
    left_all[1, :, own_cols] = (left - left_top.astype(F32)).astype(BF16)

    @pl.loop(1, chunks)
    def _(j):
        for copy in inputs(j):
            copy.wait()
        other_products(j - 1)
        cross_product(j - 1)
        energies(j)

        @pl.when(j == START)
        def _():
            pl.semaphore_wait(barrier, 127)
            left_outer().start()
            left_pair().start()
            for i in range(START - 1):
                pair_copy(i).start()

        @pl.when(j >= START)
        def _():
            pair_copy(j - 1).start()

        for i, step in enumerate(CROSSING):
            if step < chunks:

                @pl.when(j == step)
                def _(i=i):
                    pass_on(i)

    cross_product(chunks - 1)

    for n in range(128):
        cross_send[n] = cross_acc[pl.ds(n * 4, 4), :].astype(BF16)
    for d in OTHERS:
        where = place(d)
        remote(
            cross_send.at[where[0] * 32 + where[1]], cross_recv.at[snap, pts], cross_sems, 0, 1, where
        ).start()
    pltpu.make_async_copy(cross_send.at[me], cross_recv.at[snap, pts], cross_sems.at[1]).start()

    other_products(chunks - 1)
    pair_copy(chunks - 1).start()

    for n in range(32):
        rows, cols = pl.ds(n // 2 * 8, 8), pl.ds(n % 2 * 128, 128)
        range_send[n] = range_acc[rows, cols].astype(BF16)
    for d in SAME_SNAP:
        where = place(d)
        remote(range_send.at[where[1]], range_recv.at[pts], range_sems, 0, 1, where).start()
    pltpu.make_async_copy(range_send.at[pts], range_recv.at[pts], range_sems.at[1]).start()

    left_outer().wait_recv()
    left_relay().start()

    for i, step in enumerate(CROSSING):
        if step == chunks:
            pass_on(i)

    row = lax.broadcasted_iota(jnp.int32, (512, 512), 0)
    col = lax.broadcasted_iota(jnp.int32, (512, 512), 1)
    source = (col & 127) // 4 * 16 + col // 128 * 4 + (col & 3)
    order[...] = jnp.where(row == source, 1.0, 0.0).astype(BF16)

    left_pair().wait_recv()
    left_relay().wait_recv()

    remote(cross_recv, cross_recv, cross_sems, 0, 1, pair).wait_recv()
    total = jnp.concatenate([jnp.sum(cross_recv[s].astype(F32), axis=0) for s in range(4)], axis=1)
    low = total - total.astype(BF16).astype(F32)
    both = jnp.concatenate([total, low], axis=0).astype(BF16)
    top = lax.dot_general(both, left_all[0], NT, preferred_element_type=F32)
    bottom = lax.dot_general(both, left_all[1], NT, preferred_element_type=F32)
    share = top[0:4] + (top[4:8] + bottom[0:4])
    core_piece[...] = jnp.concatenate(
        [share[:, k * 128 : k * 128 + 128] for k in range(4)], axis=0
    ).astype(BF16)
    slot = z_lo * 32 + pts
    for d in SAME_CORE:
        remote(core_piece, core_all.at[core, slot], core_sems, 0, 1, place(d)).start()
    pltpu.make_async_copy(core_piece, core_all.at[core, slot], core_sems.at[1]).start()

    for i, step in enumerate(CROSSING):
        if step > chunks:
            pass_on(i)

    remote(range_recv, range_recv, range_sems, 0, 1, pair).wait_recv()
    range_piece[...] = jnp.sum(range_recv[...].astype(F32), axis=0).astype(BF16)
    for d in SAME_SNAP:
        remote(range_piece, range_all.at[pts], range_sems, 2, 3, place(d)).start()
    pltpu.make_async_copy(range_piece, range_all.at[pts], range_sems.at[3]).start()

    @pl.loop(0, chunks)
    def _(j):
        far_copy(j).wait_recv()
        cols = columns(j)
        own_acc[:, cols] = (
            own_acc[:, cols] + pair_recv[j, 0].astype(F32) + far_recv[j].astype(F32)
        )

    remote(core_all.at[core], core_all.at[core], core_sems, 0, 1, pair).wait_recv()
    relay = remote(core_all.at[core], core_all.at[core], core_sems, 2, 3, pair)
    relay.start()

    def arrange(which):
        for half in range(2):
            block = core_all[which, pl.ds(half * 32, 32)].reshape(512, 128)
            turned = lax.dot_general(
                block, order[...], (((0,), (0,)), ((), ())), preferred_element_type=F32
            )
            cols = pl.ds(pl.multiple_of((half * 2 + which) * 128, 128), 128)
            for k in range(4):
                core_sum[pl.ds(k * 128, 128), cols] = turned[:, k * 128 : k * 128 + 128]

    arrange(core)
    remote(range_all, range_all, range_sems, 2, 3, pair).wait_recv()
    for n in range(32):
        rows, cols = pl.ds(n // 2 * 8, 8), pl.ds(n % 2 * 128, 128)
        range_sum[rows, cols] = range_all[n].astype(F32)
    relay.wait_recv()
    arrange(1 - core)

    left_outer().wait_send()
    left_pair().wait_send()
    left_relay().wait_send()
    sent = cross_send.at[pl.ds(0, 127)]
    remote(sent, sent, cross_sems, 0, 1, pair).wait_send()
    sent = range_send.at[pl.ds(0, 31)]
    remote(sent, sent, range_sems, 0, 1, pair).wait_send()
    remote(sent, sent, range_sems, 2, 3, pair).wait_send()
    sent = core_all.at[0, pl.ds(0, 63)]
    remote(sent, sent, core_sems, 0, 1, pair).wait_send()
    relay.wait_send()

    @pl.loop(0, chunks)
    def _(j):
        pair_copy(j).wait_send()
        far_copy(j).wait_send()


def write_out(range_sum, own, core, range_out, own_out, core_out, sems):
    pairs = ((core, core_out), (own, own_out), (range_sum, range_out))
    copies = [pltpu.make_async_copy(a, b, sems.at[n]) for n, (a, b) in enumerate(pairs)]
    for copy in copies:
        copy.start()
    for copy in copies:
        copy.wait()


def per_device(strains, moduli, range_test, corange_test, core_left, core_right):
    points = strains.shape[2]
    chunks = points // CHUNK
    any_spec = pl.BlockSpec(memory_space=pl.ANY)
    dma = pltpu.SemaphoreType.DMA
    vmem = pltpu.VMEM
    vmem_spec = pl.BlockSpec(memory_space=pltpu.VMEM)
    own, range_sum, core = pl.pallas_call(
        kernel,
        out_shape=(
            vmem((64, points), F32),
            vmem((128, 256), F32),
            vmem((512, 512), F32),
        ),
        in_specs=[any_spec] * 6,
        out_specs=(vmem_spec,) * 3,
        scratch_shapes=[
            vmem((chunks, 6, 128, CHUNK), BF16),
            vmem((chunks, 2, CHUNK), F32),
            vmem((chunks, CHUNK, 256), BF16),
            vmem((chunks, 512, CHUNK), BF16),
            vmem((256, 128), BF16),
            vmem((512, 128), F32),
            vmem((2, 512, 512), BF16),
            vmem((chunks, 128, CHUNK), BF16),
            vmem((512, 128), F32),
            vmem((128, 256), F32),
            vmem((chunks, 64, CHUNK), F32),
            vmem((chunks, 2, 64, CHUNK), BF16),
            vmem((chunks, 2, 64, CHUNK), BF16),
            vmem((chunks, 64, CHUNK), BF16),
            vmem((chunks, 64, CHUNK), BF16),
            vmem((128, 4, 128), BF16),
            vmem((4, 32, 4, 128), BF16),
            vmem((32, 8, 128), BF16),
            vmem((32, 8, 128), BF16),
            vmem((8, 128), BF16),
            vmem((32, 8, 128), BF16),
            vmem((16, 128), BF16),
            vmem((2, 64, 16, 128), BF16),
            vmem((512, 512), BF16),
            dma((4, chunks)),
            dma((5,)),
            dma((chunks,)),
            dma((chunks,)),
            dma((chunks,)),
            dma((chunks,)),
            dma((6,)),
            dma((2,)),
            dma((4,)),
            dma((4,)),
        ],
        compiler_params=pltpu.CompilerParams(collective_id=0, has_side_effects=True),
    )(strains, moduli, range_test, corange_test, core_left, core_right)
    staged = [pltpu.with_memory_space_constraint(a, vmem) for a in (range_sum, own, core)]
    return pl.pallas_call(
        write_out,
        out_shape=[jax.ShapeDtypeStruct(a.shape, F32) for a in (range_sum, own, core)],
        in_specs=[vmem_spec] * 3,
        out_specs=[any_spec] * 3,
        scratch_shapes=[dma((3,))],
    )(*staged)


def solution(mesh):
    in_specs = (
        P(None, "snap", "pts"),
        P(None, "pts"),
        P("pts", None),
        P(),
        P(None, "snap"),
        P(None, "pts"),
    )
    out_specs = (P("snap", None), P("snap", "pts"), P())
    return jax.shard_map(
        per_device, mesh=mesh, in_specs=in_specs, out_specs=out_specs, check_vma=False
    )
```

```python
import jax
import jax.numpy as jnp
from jax import lax
from jax.experimental import pallas as pl
from jax.experimental.pallas import tpu as pltpu
from jax.sharding import PartitionSpec as P

MESH = pl.DeviceIdType.MESH
F32 = jnp.float32
BF16 = jnp.bfloat16
NT = (((1,), (1,)), ((), ()))

CHUNK = 512
START = 2
CROSSING = (3, 3, 4, 5, 8, 8, 8, 8)

ROOT = (
    0.5000000397996354,
    2 * 0.2499888951698186,
    -4 * 0.18699047969551208,
    8 * 0.24102109068796812,
    -16 * 0.3308495451729968,
    32 * 0.3494727775510849,
    -64 * 0.18534731636945423,
)
TINY = 1e-36


def hops(d):
    return sum(min(v, 4 - v) for v in d[:3])


OTHERS = sorted(
    (
        (dx, dy, dz, dc)
        for dx in range(4)
        for dy in range(4)
        for dz in range(4)
        for dc in range(2)
        if (dx, dy, dz, dc) != (0, 0, 0, 0)
    ),
    key=hops,
    reverse=True,
)
SAME_CORE = [d for d in OTHERS if d[3] == 0]
SAME_SNAP = [d for d in SAME_CORE if d[2] in (0, 2)]


def energy_tile(xx, yy, zz, xy, yz, xz, half_lame, shear):
    trace = xx + yy + zz
    mean = trace * (1.0 / 3.0)
    a = xx - mean
    b = yy - mean
    c = zz - mean
    ac = a * c
    d2 = xy * xy
    e2 = yz * yz
    f2 = xz * xz
    j2 = jnp.maximum((b * b - ac) + ((d2 + e2) + f2), TINY)
    half_det = 0.5 * (b * (ac - f2) - (a * e2 + c * d2)) + (xy * yz) * xz
    inv = lax.rsqrt(j2)
    ratio = (jnp.abs(half_det) * inv) * (inv * inv)
    root = jnp.full_like(ratio, ROOT[-1])
    for coef in ROOT[-2::-1]:
        root = root * ratio + coef
    outer = (j2 * inv) * root
    rest = jnp.maximum(j2 - 3.0 * (outer * outer), TINY)
    split = rest * lax.rsqrt(rest)
    outer = jnp.where(half_det < 0.0, -outer, outer)
    middle = mean - outer
    lone = jnp.maximum(mean + (outer + outer), 0.0)
    upper = jnp.maximum(middle + split, 0.0)
    lower = jnp.maximum(middle - split, 0.0)
    positive = jnp.maximum(trace, 0.0)
    squares = lone * lone + upper * upper + lower * lower
    return half_lame * (positive * positive) + shear * squares


def kernel(
    strains_hbm, moduli_hbm, range_hbm, corange_hbm, left_hbm, right_hbm,
    own_acc, range_sum, core_sum,
    strains, moduli, range_w, right_w, corange_w, left_w, left_all, energy_even, energy_odd,
    cross_acc, range_acc, far_acc, pair_send, pair_recv, far_send, far_recv,
    cross_send, cross_recv, range_send, range_recv, range_piece, range_all,
    core_piece, core_all, order,
    in_sems, w_sems, pair_ssem, pair_rsem, far_ssem, far_rsem,
    left_sems, cross_sems, range_sems, core_sems,
):
    snap = lax.axis_index("snap")
    pts = lax.axis_index("pts")
    z_lo = snap // 2
    core = snap % 2
    z = pts // 16 * 2 + z_lo
    x = (pts // 4) % 4
    y = pts % 4

    def place(d):
        zz = (z + d[2]) % 4
        to_snap = zz % 2 * 2 + (core + d[3]) % 2
        return to_snap, zz // 2 * 16 + (x + d[0]) % 4 * 4 + (y + d[1]) % 4

    def device(where):
        return {"snap": where[0], "pts": where[1]}

    pair = (z_lo * 2 + (1 - core), pts)
    far_snap = (1 - z_lo) * 2 + core
    far = (far_snap, pts)
    outer_z = (z + 3 + 2 * z_lo) % 4
    outer = (far_snap, outer_z // 2 * 16 + pts % 16)

    def remote(src, dst, sems, send, recv, where):
        return pltpu.make_async_remote_copy(
            src_ref=src,
            dst_ref=dst,
            send_sem=sems.at[send],
            recv_sem=sems.at[recv],
            device_id=device(where),
            device_id_type=MESH,
        )

    chunks = strains.shape[0]

    def columns(j):
        return pl.ds(j * CHUNK, CHUNK)

    def inputs(j):
        cols = columns(j)
        return (
            pltpu.make_async_copy(strains_hbm.at[:, :, cols], strains.at[j], in_sems.at[0, j]),
            pltpu.make_async_copy(moduli_hbm.at[:, cols], moduli.at[j], in_sems.at[1, j]),
            pltpu.make_async_copy(right_hbm.at[:, cols], right_w.at[j], in_sems.at[2, j]),
            pltpu.make_async_copy(range_hbm.at[cols, :], range_w.at[j], in_sems.at[3, j]),
        )

    weights = []
    own_cols = pl.ds(pl.multiple_of(snap * 128, 128), 128)
    pair_far = (1 - z_lo) * 2 + (1 - core)
    for n, owner in enumerate((snap, far_snap, pair[0], pair_far)):
        rows = pl.ds(pl.multiple_of(owner * 64, 64), 64)
        weights.append(
            pltpu.make_async_copy(
                corange_hbm.at[rows, own_cols], corange_w.at[pl.ds(n * 64, 64), :], w_sems.at[n]
            )
        )
    left_copy = pltpu.make_async_copy(left_hbm, left_w, w_sems.at[4])

    for copy in inputs(0):
        copy.start()
    left_copy.start()
    for copy in weights:
        copy.start()

    for j in range(1, chunks):
        for copy in inputs(j):
            copy.start()

    barrier = pltpu.get_barrier_semaphore()
    me = snap * 32 + pts

    @pl.loop(1, 128)
    def _(n):
        other = (me + n) % 128
        pl.semaphore_signal(
            barrier, inc=1, device_id=device((other // 32, other % 32)), device_id_type=MESH
        )

    cross_acc[...] = jnp.zeros_like(cross_acc)
    range_acc[...] = jnp.zeros_like(range_acc)

    def pair_copy(j):
        return pltpu.make_async_remote_copy(
            src_ref=pair_send.at[j],
            dst_ref=pair_recv.at[j],
            send_sem=pair_ssem.at[j],
            recv_sem=pair_rsem.at[j],
            device_id=device(pair),
            device_id_type=MESH,
        )

    def far_copy(j):
        return pltpu.make_async_remote_copy(
            src_ref=far_send.at[j],
            dst_ref=far_recv.at[j],
            send_sem=far_ssem.at[j],
            recv_sem=far_rsem.at[j],
            device_id=device(far),
            device_id_type=MESH,
        )

    def pass_on(j):
        pair_copy(j).wait_recv()
        far_send[j] = (far_acc[j] + pair_recv[j, 1].astype(F32)).astype(BF16)
        far_copy(j).start()

    energy = (energy_even, energy_odd)

    def energies(j):
        for lane in range(0, CHUNK, 128):
            cols = pl.ds(lane, 128)
            half_lame = 0.5 * moduli[j, 0:1, cols]
            shear = moduli[j, 1:2, cols]
            for row in range(0, 128, 16):
                rows = pl.ds(row, 16)
                parts = [strains[j, k, rows, cols].astype(F32) for k in range(6)]
                energy[j % 2][rows, cols] = energy_tile(*parts, half_lame, shear).astype(BF16)

    def cross_product(j):
        cross_acc[...] += lax.dot_general(right_w[j], energy[j % 2][...], NT, preferred_element_type=F32)

    def other_products(j):
        field = energy[j % 2][...]
        own = jnp.dot(corange_w[...], field, preferred_element_type=F32)
        own_acc[:, columns(j)] = own[:64]
        far_acc[j] = own[64:128]
        pair_send[j, 0] = own[128:192].astype(BF16)
        pair_send[j, 1] = own[192:].astype(BF16)
        range_acc[...] += jnp.dot(field, range_w[j], preferred_element_type=F32)

    def left_slot(s):
        return left_all.at[:, :, pl.ds(pl.multiple_of(s * 128, 128), 128)]

    def left_pair():
        return remote(left_slot(snap), left_slot(snap), left_sems, 0, 1, pair)

    def left_outer():
        return remote(left_slot(snap), left_slot(snap), left_sems, 2, 3, outer)

    def left_relay():
        return remote(left_slot(far_snap), left_slot(far_snap), left_sems, 4, 5, pair)

    for copy in inputs(0):
        copy.wait()
    energies(0)
    for copy in weights:
        copy.wait()
    left_copy.wait()
    left = left_w[...]
    left_top = left.astype(BF16)
    left_all[0, :, own_cols] = left_top
    left_all[1, :, own_cols] = (left - left_top.astype(F32)).astype(BF16)

    for j in range(1, chunks):
        for copy in inputs(j):
            copy.wait()
        other_products(j - 1)
        cross_product(j - 1)
        energies(j)
        if j == START:
            pl.semaphore_wait(barrier, 127)
            left_outer().start()
            left_pair().start()
            for i in range(START - 1):
                pair_copy(i).start()
        if j >= START:
            pair_copy(j - 1).start()
        for i, step in enumerate(CROSSING):
            if step == j:
                pass_on(i)

    cross_product(chunks - 1)

    for n in range(128):
        cross_send[n] = cross_acc[pl.ds(n * 4, 4), :].astype(BF16)
    for d in OTHERS:
        where = place(d)
        remote(
            cross_send.at[where[0] * 32 + where[1]], cross_recv.at[snap, pts], cross_sems, 0, 1, where
        ).start()
    pltpu.make_async_copy(cross_send.at[me], cross_recv.at[snap, pts], cross_sems.at[1]).start()

    other_products(chunks - 1)
    pair_copy(chunks - 1).start()

    for n in range(32):
        rows, cols = pl.ds(n // 2 * 8, 8), pl.ds(n % 2 * 128, 128)
        range_send[n] = range_acc[rows, cols].astype(BF16)
    for d in SAME_SNAP:
        where = place(d)
        remote(range_send.at[where[1]], range_recv.at[pts], range_sems, 0, 1, where).start()
    pltpu.make_async_copy(range_send.at[pts], range_recv.at[pts], range_sems.at[1]).start()

    left_outer().wait_recv()
    left_relay().start()

    for i, step in enumerate(CROSSING):
        if step == chunks:
            pass_on(i)

    row = lax.broadcasted_iota(jnp.int32, (512, 512), 0)
    col = lax.broadcasted_iota(jnp.int32, (512, 512), 1)
    source = (col & 127) // 4 * 16 + col // 128 * 4 + (col & 3)
    order[...] = jnp.where(row == source, 1.0, 0.0).astype(BF16)

    left_pair().wait_recv()
    left_relay().wait_recv()

    remote(cross_recv, cross_recv, cross_sems, 0, 1, pair).wait_recv()
    total = jnp.concatenate([jnp.sum(cross_recv[s].astype(F32), axis=0) for s in range(4)], axis=1)
    low = total - total.astype(BF16).astype(F32)
    both = jnp.concatenate([total, low], axis=0).astype(BF16)
    top = lax.dot_general(both, left_all[0], NT, preferred_element_type=F32)
    bottom = lax.dot_general(both, left_all[1], NT, preferred_element_type=F32)
    share = top[0:4] + (top[4:8] + bottom[0:4])
    core_piece[...] = jnp.concatenate(
        [share[:, k * 128 : k * 128 + 128] for k in range(4)], axis=0
    ).astype(BF16)
    slot = z_lo * 32 + pts
    for d in SAME_CORE:
        remote(core_piece, core_all.at[core, slot], core_sems, 0, 1, place(d)).start()
    pltpu.make_async_copy(core_piece, core_all.at[core, slot], core_sems.at[1]).start()

    for i, step in enumerate(CROSSING):
        if step > chunks:
            pass_on(i)

    remote(range_recv, range_recv, range_sems, 0, 1, pair).wait_recv()
    range_piece[...] = jnp.sum(range_recv[...].astype(F32), axis=0).astype(BF16)
    for d in SAME_SNAP:
        remote(range_piece, range_all.at[pts], range_sems, 2, 3, place(d)).start()
    pltpu.make_async_copy(range_piece, range_all.at[pts], range_sems.at[3]).start()

    for j in range(chunks):
        far_copy(j).wait_recv()
        cols = columns(j)
        own_acc[:, cols] = (
            own_acc[:, cols] + pair_recv[j, 0].astype(F32) + far_recv[j].astype(F32)
        )

    remote(core_all.at[core], core_all.at[core], core_sems, 0, 1, pair).wait_recv()
    relay = remote(core_all.at[core], core_all.at[core], core_sems, 2, 3, pair)
    relay.start()

    def arrange(which):
        for half in range(2):
            block = core_all[which, pl.ds(half * 32, 32)].reshape(512, 128)
            turned = lax.dot_general(
                block, order[...], (((0,), (0,)), ((), ())), preferred_element_type=F32
            )
            cols = pl.ds(pl.multiple_of((half * 2 + which) * 128, 128), 128)
            for k in range(4):
                core_sum[pl.ds(k * 128, 128), cols] = turned[:, k * 128 : k * 128 + 128]

    arrange(core)
    remote(range_all, range_all, range_sems, 2, 3, pair).wait_recv()
    for n in range(32):
        rows, cols = pl.ds(n // 2 * 8, 8), pl.ds(n % 2 * 128, 128)
        range_sum[rows, cols] = range_all[n].astype(F32)
    relay.wait_recv()
    arrange(1 - core)

    left_outer().wait_send()
    left_pair().wait_send()
    left_relay().wait_send()
    sent = cross_send.at[pl.ds(0, 127)]
    remote(sent, sent, cross_sems, 0, 1, pair).wait_send()
    sent = range_send.at[pl.ds(0, 31)]
    remote(sent, sent, range_sems, 0, 1, pair).wait_send()
    remote(sent, sent, range_sems, 2, 3, pair).wait_send()
    sent = core_all.at[0, pl.ds(0, 63)]
    remote(sent, sent, core_sems, 0, 1, pair).wait_send()
    relay.wait_send()

    @pl.loop(0, chunks)
    def _(j):
        pair_copy(j).wait_send()
        far_copy(j).wait_send()


def write_out(range_sum, own, core, range_out, own_out, core_out, sems):
    pairs = ((core, core_out), (own, own_out), (range_sum, range_out))
    copies = [pltpu.make_async_copy(a, b, sems.at[n]) for n, (a, b) in enumerate(pairs)]
    for copy in copies:
        copy.start()
    for copy in copies:
        copy.wait()


def per_device(strains, moduli, range_test, corange_test, core_left, core_right):
    points = strains.shape[2]
    chunks = points // CHUNK
    any_spec = pl.BlockSpec(memory_space=pl.ANY)
    dma = pltpu.SemaphoreType.DMA
    vmem = pltpu.VMEM
    vmem_spec = pl.BlockSpec(memory_space=pltpu.VMEM)
    own, range_sum, core = pl.pallas_call(
        kernel,
        out_shape=(
            vmem((64, points), F32),
            vmem((128, 256), F32),
            vmem((512, 512), F32),
        ),
        in_specs=[any_spec] * 6,
        out_specs=(vmem_spec,) * 3,
        scratch_shapes=[
            vmem((chunks, 6, 128, CHUNK), BF16),
            vmem((chunks, 2, CHUNK), F32),
            vmem((chunks, CHUNK, 256), BF16),
            vmem((chunks, 512, CHUNK), BF16),
            vmem((256, 128), BF16),
            vmem((512, 128), F32),
            vmem((2, 512, 512), BF16),
            vmem((128, CHUNK), BF16),
            vmem((128, CHUNK), BF16),
            vmem((512, 128), F32),
            vmem((128, 256), F32),
            vmem((chunks, 64, CHUNK), F32),
            vmem((chunks, 2, 64, CHUNK), BF16),
            vmem((chunks, 2, 64, CHUNK), BF16),
            vmem((chunks, 64, CHUNK), BF16),
            vmem((chunks, 64, CHUNK), BF16),
            vmem((128, 4, 128), BF16),
            vmem((4, 32, 4, 128), BF16),
            vmem((32, 8, 128), BF16),
            vmem((32, 8, 128), BF16),
            vmem((8, 128), BF16),
            vmem((32, 8, 128), BF16),
            vmem((16, 128), BF16),
            vmem((2, 64, 16, 128), BF16),
            vmem((512, 512), BF16),
            dma((4, chunks)),
            dma((5,)),
            dma((chunks,)),
            dma((chunks,)),
            dma((chunks,)),
            dma((chunks,)),
            dma((6,)),
            dma((2,)),
            dma((4,)),
            dma((4,)),
        ],
        compiler_params=pltpu.CompilerParams(collective_id=0, has_side_effects=True),
    )(strains, moduli, range_test, corange_test, core_left, core_right)
    staged = [pltpu.with_memory_space_constraint(a, vmem) for a in (range_sum, own, core)]
    return pl.pallas_call(
        write_out,
        out_shape=[jax.ShapeDtypeStruct(a.shape, F32) for a in (range_sum, own, core)],
        in_specs=[vmem_spec] * 3,
        out_specs=[any_spec] * 3,
        scratch_shapes=[dma((3,))],
    )(*staged)


def solution(mesh):
    in_specs = (
        P(None, "snap", "pts"),
        P(None, "pts"),
        P("pts", None),
        P(),
        P(None, "snap"),
        P(None, "pts"),
    )
    out_specs = (P("snap", None), P("snap", "pts"), P())
    return jax.shard_map(
        per_device, mesh=mesh, in_specs=in_specs, out_specs=out_specs, check_vma=False
    )
```

```python
import jax
import jax.numpy as jnp
from jax import lax
from jax.experimental import pallas as pl
from jax.experimental.pallas import tpu as pltpu
from jax.sharding import PartitionSpec as P

MESH = pl.DeviceIdType.MESH
F32 = jnp.float32
BF16 = jnp.bfloat16
NT = (((1,), (1,)), ((), ()))

CHUNK = 512
START = 2
CROSSING = (3, 3, 4, 5, 8, 8, 8, 8)

ROOT = (
    0.5000000397996354,
    2 * 0.2499888951698186,
    -4 * 0.18699047969551208,
    8 * 0.24102109068796812,
    -16 * 0.3308495451729968,
    32 * 0.3494727775510849,
    -64 * 0.18534731636945423,
)
TINY = 1e-36


def hops(d):
    return sum(min(v, 4 - v) for v in d[:3])


OTHERS = sorted(
    (
        (dx, dy, dz, dc)
        for dx in range(4)
        for dy in range(4)
        for dz in range(4)
        for dc in range(2)
        if (dx, dy, dz, dc) != (0, 0, 0, 0)
    ),
    key=hops,
    reverse=True,
)
SAME_CORE = [d for d in OTHERS if d[3] == 0]
SAME_SNAP = [d for d in SAME_CORE if d[2] in (0, 2)]


def energy_tile(xx, yy, zz, xy, yz, xz, half_lame, shear):
    trace = xx + yy + zz
    mean = trace * (1.0 / 3.0)
    a = xx - mean
    b = yy - mean
    c = zz - mean
    ac = a * c
    d2 = xy * xy
    e2 = yz * yz
    f2 = xz * xz
    j2 = jnp.maximum((b * b - ac) + ((d2 + e2) + f2), TINY)
    half_det = 0.5 * (b * (ac - f2) - (a * e2 + c * d2)) + (xy * yz) * xz
    inv = lax.rsqrt(j2)
    ratio = (jnp.abs(half_det) * inv) * (inv * inv)
    root = jnp.full_like(ratio, ROOT[-1])
    for coef in ROOT[-2::-1]:
        root = root * ratio + coef
    outer = (j2 * inv) * root
    rest = jnp.maximum(j2 - 3.0 * (outer * outer), TINY)
    split = rest * lax.rsqrt(rest)
    outer = jnp.where(half_det < 0.0, -outer, outer)
    middle = mean - outer
    lone = jnp.maximum(mean + (outer + outer), 0.0)
    upper = jnp.maximum(middle + split, 0.0)
    lower = jnp.maximum(middle - split, 0.0)
    positive = jnp.maximum(trace, 0.0)
    squares = lone * lone + upper * upper + lower * lower
    return half_lame * (positive * positive) + shear * squares


def kernel(
    strains_hbm, moduli_hbm, range_hbm, corange_hbm, left_hbm, right_hbm,
    own_acc, range_sum, core_sum,
    strains, moduli, range_w, right_w, corange_w, left_w, left_all, energy_even, energy_odd,
    cross_acc, range_acc, far_acc, pair_send, pair_recv, far_send, far_recv,
    cross_send, cross_recv, range_send, range_recv, range_piece, range_all,
    core_piece, core_all, order,
    in_sems, w_sems, pair_ssem, pair_rsem, far_ssem, far_rsem,
    left_sems, cross_sems, range_sems, core_sems,
):
    snap = lax.axis_index("snap")
    pts = lax.axis_index("pts")
    z_lo = snap // 2
    core = snap % 2
    z = pts // 16 * 2 + z_lo
    x = (pts // 4) % 4
    y = pts % 4

    def place(d):
        zz = (z + d[2]) % 4
        to_snap = zz % 2 * 2 + (core + d[3]) % 2
        return to_snap, zz // 2 * 16 + (x + d[0]) % 4 * 4 + (y + d[1]) % 4

    def device(where):
        return {"snap": where[0], "pts": where[1]}

    pair = (z_lo * 2 + (1 - core), pts)
    far_snap = (1 - z_lo) * 2 + core
    far = (far_snap, pts)
    outer_z = (z + 3 + 2 * z_lo) % 4
    outer = (far_snap, outer_z // 2 * 16 + pts % 16)

    def remote(src, dst, sems, send, recv, where):
        return pltpu.make_async_remote_copy(
            src_ref=src,
            dst_ref=dst,
            send_sem=sems.at[send],
            recv_sem=sems.at[recv],
            device_id=device(where),
            device_id_type=MESH,
        )

    chunks = strains.shape[0]

    def columns(j):
        return pl.ds(j * CHUNK, CHUNK)

    def inputs(j):
        cols = columns(j)
        return (
            pltpu.make_async_copy(strains_hbm.at[:, :, cols], strains.at[j], in_sems.at[0, j]),
            pltpu.make_async_copy(moduli_hbm.at[:, cols], moduli.at[j], in_sems.at[1, j]),
            pltpu.make_async_copy(right_hbm.at[:, cols], right_w.at[j], in_sems.at[2, j]),
            pltpu.make_async_copy(range_hbm.at[cols, :], range_w.at[j], in_sems.at[3, j]),
        )

    weights = []
    own_cols = pl.ds(pl.multiple_of(snap * 128, 128), 128)
    pair_far = (1 - z_lo) * 2 + (1 - core)
    for n, owner in enumerate((snap, far_snap, pair[0], pair_far)):
        rows = pl.ds(pl.multiple_of(owner * 64, 64), 64)
        weights.append(
            pltpu.make_async_copy(
                corange_hbm.at[rows, own_cols], corange_w.at[pl.ds(n * 64, 64), :], w_sems.at[n]
            )
        )
    left_copy = pltpu.make_async_copy(left_hbm, left_w, w_sems.at[4])

    for copy in inputs(0):
        copy.start()
    left_copy.start()
    for copy in weights:
        copy.start()

    for j in range(1, chunks):
        for copy in inputs(j):
            copy.start()

    barrier = pltpu.get_barrier_semaphore()
    me = snap * 32 + pts

    @pl.loop(1, 128)
    def _(n):
        other = (me + n) % 128
        pl.semaphore_signal(
            barrier, inc=1, device_id=device((other // 32, other % 32)), device_id_type=MESH
        )

    cross_acc[...] = jnp.zeros_like(cross_acc)
    range_acc[...] = jnp.zeros_like(range_acc)

    def pair_copy(j):
        return pltpu.make_async_remote_copy(
            src_ref=pair_send.at[j],
            dst_ref=pair_recv.at[j],
            send_sem=pair_ssem.at[j],
            recv_sem=pair_rsem.at[j],
            device_id=device(pair),
            device_id_type=MESH,
        )

    def far_copy(j):
        return pltpu.make_async_remote_copy(
            src_ref=far_send.at[j],
            dst_ref=far_recv.at[j],
            send_sem=far_ssem.at[j],
            recv_sem=far_rsem.at[j],
            device_id=device(far),
            device_id_type=MESH,
        )

    def pass_on(j):
        pair_copy(j).wait_recv()
        far_send[j] = (far_acc[j] + pair_recv[j, 1].astype(F32)).astype(BF16)
        far_copy(j).start()

    energy = (energy_even, energy_odd)

    def energies(j):
        for lane in range(0, CHUNK, 128):
            cols = pl.ds(lane, 128)
            half_lame = 0.5 * moduli[j, 0:1, cols]
            shear = moduli[j, 1:2, cols]
            for row in range(0, 128, 16):
                rows = pl.ds(row, 16)
                parts = [strains[j, k, rows, cols].astype(F32) for k in range(6)]
                energy[j % 2][rows, cols] = energy_tile(*parts, half_lame, shear).astype(BF16)

    def cross_product(j):
        field = energy[j % 2][...]
        for half in range(2):
            rows = pl.ds(half * 256, 256)
            cross_acc[rows, :] += lax.dot_general(
                right_w[j, rows, :], field, NT, preferred_element_type=F32
            )

    def other_products(j):
        field = energy[j % 2][...]
        own = jnp.dot(corange_w[...], field, preferred_element_type=F32)
        own_acc[:, columns(j)] = own[:64]
        far_acc[j] = own[64:128]
        pair_send[j, 0] = own[128:192].astype(BF16)
        pair_send[j, 1] = own[192:].astype(BF16)
        range_acc[...] += jnp.dot(field, range_w[j], preferred_element_type=F32)

    def left_slot(s):
        return left_all.at[:, :, pl.ds(pl.multiple_of(s * 128, 128), 128)]

    def left_pair():
        return remote(left_slot(snap), left_slot(snap), left_sems, 0, 1, pair)

    def left_outer():
        return remote(left_slot(snap), left_slot(snap), left_sems, 2, 3, outer)

    def left_relay():
        return remote(left_slot(far_snap), left_slot(far_snap), left_sems, 4, 5, pair)

    for copy in inputs(0):
        copy.wait()
    energies(0)
    for copy in weights:
        copy.wait()
    left_copy.wait()
    left = left_w[...]
    left_top = left.astype(BF16)
    left_all[0, :, own_cols] = left_top
    left_all[1, :, own_cols] = (left - left_top.astype(F32)).astype(BF16)

    for j in range(1, chunks):
        for copy in inputs(j):
            copy.wait()
        other_products(j - 1)
        cross_product(j - 1)
        energies(j)
        if j == START:
            pl.semaphore_wait(barrier, 127)
            left_outer().start()
            left_pair().start()
            for i in range(START - 1):
                pair_copy(i).start()
        if j >= START:
            pair_copy(j - 1).start()
        for i, step in enumerate(CROSSING):
            if step == j:
                pass_on(i)

    cross_product(chunks - 1)

    for n in range(128):
        cross_send[n] = cross_acc[pl.ds(n * 4, 4), :].astype(BF16)
    for d in OTHERS:
        where = place(d)
        remote(
            cross_send.at[where[0] * 32 + where[1]], cross_recv.at[snap, pts], cross_sems, 0, 1, where
        ).start()
    pltpu.make_async_copy(cross_send.at[me], cross_recv.at[snap, pts], cross_sems.at[1]).start()

    other_products(chunks - 1)
    pair_copy(chunks - 1).start()

    for n in range(32):
        rows, cols = pl.ds(n // 2 * 8, 8), pl.ds(n % 2 * 128, 128)
        range_send[n] = range_acc[rows, cols].astype(BF16)
    for d in SAME_SNAP:
        where = place(d)
        remote(range_send.at[where[1]], range_recv.at[pts], range_sems, 0, 1, where).start()
    pltpu.make_async_copy(range_send.at[pts], range_recv.at[pts], range_sems.at[1]).start()

    left_outer().wait_recv()
    left_relay().start()

    for i, step in enumerate(CROSSING):
        if step == chunks:
            pass_on(i)

    row = lax.broadcasted_iota(jnp.int32, (512, 512), 0)
    col = lax.broadcasted_iota(jnp.int32, (512, 512), 1)
    source = (col & 127) // 4 * 16 + col // 128 * 4 + (col & 3)
    order[...] = jnp.where(row == source, 1.0, 0.0).astype(BF16)

    left_pair().wait_recv()
    left_relay().wait_recv()

    remote(cross_recv, cross_recv, cross_sems, 0, 1, pair).wait_recv()
    total = jnp.concatenate([jnp.sum(cross_recv[s].astype(F32), axis=0) for s in range(4)], axis=1)
    low = total - total.astype(BF16).astype(F32)
    both = jnp.concatenate([total, low], axis=0).astype(BF16)
    top = lax.dot_general(both, left_all[0], NT, preferred_element_type=F32)
    bottom = lax.dot_general(both, left_all[1], NT, preferred_element_type=F32)
    share = top[0:4] + (top[4:8] + bottom[0:4])
    core_piece[...] = jnp.concatenate(
        [share[:, k * 128 : k * 128 + 128] for k in range(4)], axis=0
    ).astype(BF16)
    slot = z_lo * 32 + pts
    for d in SAME_CORE:
        remote(core_piece, core_all.at[core, slot], core_sems, 0, 1 + d[2] % 2, place(d)).start()
    pltpu.make_async_copy(core_piece, core_all.at[core, slot], core_sems.at[1]).start()

    for i, step in enumerate(CROSSING):
        if step > chunks:
            pass_on(i)

    remote(range_recv, range_recv, range_sems, 0, 1, pair).wait_recv()
    range_piece[...] = jnp.sum(range_recv[...].astype(F32), axis=0).astype(BF16)
    for d in SAME_SNAP:
        remote(range_piece, range_all.at[pts], range_sems, 2, 3, place(d)).start()
    pltpu.make_async_copy(range_piece, range_all.at[pts], range_sems.at[3]).start()

    for j in range(chunks):
        far_copy(j).wait_recv()
        cols = columns(j)
        own_acc[:, cols] = (
            own_acc[:, cols] + pair_recv[j, 0].astype(F32) + far_recv[j].astype(F32)
        )

    def half_of(which, half):
        return core_all.at[which, pl.ds(pl.multiple_of(half * 32, 32), 32)]

    def arrived(half, recv):
        ref = half_of(core, half)
        remote(ref, ref, core_sems, 0, recv, pair).wait_recv()

    def relay(half, n):
        ref = half_of(core, half)
        return remote(ref, ref, core_sems, 3 + n, 5 + n, pair)

    def arrange(which, half):
        block = half_of(which, half)[...].reshape(512, 128)
        turned = lax.dot_general(
            block, order[...], (((0,), (0,)), ((), ())), preferred_element_type=F32
        )
        cols = pl.ds(pl.multiple_of((half * 2 + which) * 128, 128), 128)
        for k in range(4):
            core_sum[pl.ds(k * 128, 128), cols] = turned[:, k * 128 : k * 128 + 128]

    first, second = 1 - z_lo, z_lo
    arrived(first, 2)
    relay(first, 0).start()
    arrange(core, first)
    arrived(second, 1)
    relay(second, 1).start()
    arrange(core, second)
    remote(range_all, range_all, range_sems, 2, 3, pair).wait_recv()
    for n in range(32):
        rows, cols = pl.ds(n // 2 * 8, 8), pl.ds(n % 2 * 128, 128)
        range_sum[rows, cols] = range_all[n].astype(F32)
    relay(first, 0).wait_recv()
    arrange(1 - core, first)
    relay(second, 1).wait_recv()
    arrange(1 - core, second)

    left_outer().wait_send()
    left_pair().wait_send()
    left_relay().wait_send()
    sent = cross_send.at[pl.ds(0, 127)]
    remote(sent, sent, cross_sems, 0, 1, pair).wait_send()
    sent = range_send.at[pl.ds(0, 31)]
    remote(sent, sent, range_sems, 0, 1, pair).wait_send()
    remote(sent, sent, range_sems, 2, 3, pair).wait_send()
    sent = core_all.at[0, pl.ds(0, 63)]
    remote(sent, sent, core_sems, 0, 1, pair).wait_send()
    relay(first, 0).wait_send()
    relay(second, 1).wait_send()

    @pl.loop(0, chunks)
    def _(j):
        pair_copy(j).wait_send()
        far_copy(j).wait_send()


def write_out(range_sum, own, core, range_out, own_out, core_out, sems):
    pairs = ((core, core_out), (own, own_out), (range_sum, range_out))
    copies = [pltpu.make_async_copy(a, b, sems.at[n]) for n, (a, b) in enumerate(pairs)]
    for copy in copies:
        copy.start()
    for copy in copies:
        copy.wait()


def per_device(strains, moduli, range_test, corange_test, core_left, core_right):
    points = strains.shape[2]
    chunks = points // CHUNK
    any_spec = pl.BlockSpec(memory_space=pl.ANY)
    dma = pltpu.SemaphoreType.DMA
    vmem = pltpu.VMEM
    vmem_spec = pl.BlockSpec(memory_space=pltpu.VMEM)
    own, range_sum, core = pl.pallas_call(
        kernel,
        out_shape=(
            vmem((64, points), F32),
            vmem((128, 256), F32),
            vmem((512, 512), F32),
        ),
        in_specs=[any_spec] * 6,
        out_specs=(vmem_spec,) * 3,
        scratch_shapes=[
            vmem((chunks, 6, 128, CHUNK), BF16),
            vmem((chunks, 2, CHUNK), F32),
            vmem((chunks, CHUNK, 256), BF16),
            vmem((chunks, 512, CHUNK), BF16),
            vmem((256, 128), BF16),
            vmem((512, 128), F32),
            vmem((2, 512, 512), BF16),
            vmem((128, CHUNK), BF16),
            vmem((128, CHUNK), BF16),
            vmem((512, 128), F32),
            vmem((128, 256), F32),
            vmem((chunks, 64, CHUNK), F32),
            vmem((chunks, 2, 64, CHUNK), BF16),
            vmem((chunks, 2, 64, CHUNK), BF16),
            vmem((chunks, 64, CHUNK), BF16),
            vmem((chunks, 64, CHUNK), BF16),
            vmem((128, 4, 128), BF16),
            vmem((4, 32, 4, 128), BF16),
            vmem((32, 8, 128), BF16),
            vmem((32, 8, 128), BF16),
            vmem((8, 128), BF16),
            vmem((32, 8, 128), BF16),
            vmem((16, 128), BF16),
            vmem((2, 64, 16, 128), BF16),
            vmem((512, 512), BF16),
            dma((4, chunks)),
            dma((5,)),
            dma((chunks,)),
            dma((chunks,)),
            dma((chunks,)),
            dma((chunks,)),
            dma((6,)),
            dma((2,)),
            dma((4,)),
            dma((7,)),
        ],
        compiler_params=pltpu.CompilerParams(collective_id=0, has_side_effects=True),
    )(strains, moduli, range_test, corange_test, core_left, core_right)
    staged = [pltpu.with_memory_space_constraint(a, vmem) for a in (range_sum, own, core)]
    return pl.pallas_call(
        write_out,
        out_shape=[jax.ShapeDtypeStruct(a.shape, F32) for a in (range_sum, own, core)],
        in_specs=[vmem_spec] * 3,
        out_specs=[any_spec] * 3,
        scratch_shapes=[dma((3,))],
    )(*staged)


def solution(mesh):
    in_specs = (
        P(None, "snap", "pts"),
        P(None, "pts"),
        P("pts", None),
        P(),
        P(None, "snap"),
        P(None, "pts"),
    )
    out_specs = (P("snap", None), P("snap", "pts"), P())
    return jax.shard_map(
        per_device, mesh=mesh, in_specs=in_specs, out_specs=out_specs, check_vma=False
    )
```
